128 devices in a mesh: bx: 16 (over x, y), by: 8 (over z, core).
Axes of the slice: x: 4, y: 4, z: 4, core: 2. Of those that a mesh axis runs over, the one named last changes fastest.
Arguments:
- sensitivities: float32 [32, 1048576], P(None, ('bx', 'by')), may hold values from -6 to 6
- owner: int32 [1048576, 1], P(('bx', 'by')), may hold values from 0 to 127; in each aligned block of 8192 rows (0 to 8191, 8192 to 16383, ...) at most 128 rows name the same one
- owner_cell: int32 [1048576], P(('bx', 'by')), may hold values from 0 to 2047
- leaf_factor: bfloat16 [128, 2048, 2048], P(('bx', 'by')), may hold values from -3 to 3
- coupling1: bfloat16 [262144, 512], P(('bx', 'by')), may hold values from -0.0625 to 0.0625
- coupling2: bfloat16 [262144, 1024], P(('bx', 'by')), may hold values from -0.0625 to 0.0625
- sep_coupling: bfloat16 [8192, 1024], P(('bx', 'by')), may hold values from -0.25 to 0.25
- sep1_factor: bfloat16 [8192, 512], P(('bx', 'by')), may hold values from -3 to 3
- sep2_factor: bfloat16 [1024, 1024], P(('bx', 'by')), may hold values from -3 to 3
- sep1_rhs: float32 [32, 8192], P(None, ('bx', 'by')), may hold values from -6 to 6
- sep2_rhs: float32 [32, 1024], P(None, ('bx', 'by')), may hold values from -6 to 6
Outputs:
- filtered: float32 [32, 262144], P(None, ('bx', 'by'))
- sep1_field: float32 [32, 8192], P(None, 'bx')
- sep2_field: float32 [32, 1024], replicated
The draws below stay inside these ranges and needn't reach their ends.
Inputs may be any that keep to these rules, and one draw needn't show every extreme that they name: Within the rows of one analysis owner no filter owner is named more than 128 times; some owner is named exactly 128 times in some owners' rows.
All inputs are finite; a program needn't handle non-finite values.
Results may differ from the reference program's by a relative error of at most 0.017.
Values may be sent and summed in bfloat16 or wider, within the bound.
A program may use at most 128 MiB of HBM per device.

```python
import math
import jax
import jax.numpy as jnp
import numpy as np
from jax import lax

R = 32
NI = 2048
NS1 = 512
NS2 = 1024
A_DEV = 8192
CAP = 128
N_BX = 16
N_BY = 8
DEVICES = 128


def dominant_block(key, shape, width):
    noise = jax.random.normal(key, shape, jnp.float32) * (0.5 / math.sqrt(width))
    noise = jnp.clip(noise, -2.0, 2.0)
    rows = lax_rows(shape)
    cols = jnp.arange(shape[-1], dtype=jnp.int32)
    eye = (rows % width == cols).astype(jnp.float32)
    return eye + noise


def lax_rows(shape):
    count = shape[-2]
    rows = jnp.arange(count, dtype=jnp.int32)
    return rows.reshape((count, 1))


def draw_leaf_factor(key, part):
    return dominant_block(jax.random.fold_in(key, 11), (DEVICES, NI, NI), NI).astype(jnp.bfloat16)


def draw_sep1_factor(key, part):
    return dominant_block(jax.random.fold_in(key, 12), (N_BX * NS1, NS1), NS1).astype(jnp.bfloat16)


def draw_sep2_factor(key, part):
    return dominant_block(jax.random.fold_in(key, 13), (NS2, NS2), NS2).astype(jnp.bfloat16)


def plant(array, rng, low, high):
    longest = array.shape.index(max(array.shape))
    spots = []
    for shift in (0, 1):
        where = [jax.random.randint(jax.random.fold_in(rng, axis), (), 0, length) for axis, length in enumerate(array.shape)]
        where[longest] = (where[longest] + shift) % array.shape[longest]
        spots.append(tuple(where))
    return array.at[spots[0]].set(low).at[spots[1]].set(high)


def levels(stream_key, extent, shards, smallest, largest):
    def one(position, shards_of):
        draws = jax.random.uniform(jax.random.fold_in(jax.random.fold_in(stream_key, 6), position), (shards_of,), jnp.float32, smallest / len(shards), largest / len(shards))
        return jnp.repeat(jnp.exp(draws), extent[position] // shards_of).reshape((-1,) + (1,) * (len(extent) - position - 1))

    loudness = one(*shards[0])
    for cut in shards[1:]:
        loudness = loudness * one(*cut)
    return loudness


def shared_out(key, own, number, rows, count, top, bound, lean):
    order = jax.random.permutation(key, count)
    heavy_load, usual = shares(count, rows * top, bound, lean, True), shares(count, rows * top, bound, lean, False)
    places = jnp.arange(count)

    def named(lengths, rotation):
        used = int((lengths > 0).sum())
        fixed = max(1, used // 4)
        moved = fixed + (places - fixed + rotation * (used - fixed)) % max(1, count - fixed)
        return jnp.zeros((count,), jnp.int32).at[order[jnp.where(places < fixed, places, moved)]].set(jnp.asarray(lengths, jnp.int32))

    lengths = jnp.where(number % 4 == 0, named(heavy_load, number // 4), named(usual, number - number // 4 - 1))
    mixed = jax.random.permutation(jax.random.fold_in(own, 3), count)
    giver, sink = mixed[0:count // 2 * 2:2], mixed[1:count // 2 * 2:2]
    margin = jnp.minimum(lengths[giver] - 1, bound - lengths[sink]) // 2
    margin = jnp.where((giver == order[0]) | (sink == order[0]) | (lengths[sink] == 0), 0, jnp.maximum(margin, 0))
    moved = jax.random.randint(jax.random.fold_in(own, 4), (count // 2,), 0, 1 << 20) % (margin + 1)
    lengths = lengths.at[giver].add(-moved).at[sink].add(moved)
    labels = jnp.searchsorted(jnp.cumsum(lengths), jnp.arange(rows * top), side="right").astype(jnp.int32)
    grid = labels.reshape(top, rows).T
    grid = grid[jax.random.permutation(jax.random.fold_in(own, 1), rows)]
    rotation = jax.random.randint(jax.random.fold_in(own, 2), (rows, 1), 0, top)
    return jnp.take_along_axis(grid, (jnp.arange(top)[None, :] + rotation) % top, axis=1)


def shares(number_of, total, limit, skew, full):
    loads = [(1 << 20) // math.isqrt(standing ** skew) + 1 for standing in range(1, number_of + 1)]
    largest = limit if full else min(limit, max(-(-total // number_of), total * loads[0] // sum(loads)))
    least = 1 if total - largest >= number_of - 1 else 0
    given, spare = [largest] + [least] * (number_of - 1), total - largest - least * (number_of - 1)
    while spare > 0:
        candidates = [i for i in range(1, number_of) if given[i] < largest] or [i for i in range(1, number_of) if given[i] < limit]
        pool, left = sum([loads[i] for i in candidates]), spare
        for i in candidates:
            extra = min(limit - given[i], max(1, left * loads[i] // pool), spare)
            given[i] = given[i] + extra
            spare = spare - extra
    return np.array(given)


def centred(own_key, shape, deviation, reach, cuts=(), kind=jnp.bfloat16):
    array = jax.random.normal(own_key, shape, jnp.float32) * deviation
    if len(cuts) > 0:
        array = levels(own_key, shape, cuts, -0.22, 0.18) * array
    return jnp.clip(array, min=-reach, max=reach).astype(kind)


def setup_inputs(seed: int = 0) -> dict:
    key_list = jax.random.split(jax.random.key(seed), 12)
    sensitivities = centred(key_list[0], (R, DEVICES * A_DEV), 1.0, 6.0, ((1, 128),), jnp.float32)
    owner_keys = jax.random.split(jax.random.fold_in(key_list[1], 1), (DEVICES * A_DEV) // A_DEV)
    owner_turns = jax.random.permutation(jax.random.fold_in(key_list[1], 3), (DEVICES * A_DEV) // A_DEV)
    owner = jax.vmap(lambda own, number: shared_out(jax.random.fold_in(key_list[1], 2), own, number, A_DEV, DEVICES, 1, CAP, 2))(owner_keys, owner_turns).reshape((DEVICES * A_DEV, 1))
    owner_cell = plant(jax.random.randint(key_list[2], (DEVICES * A_DEV,), 0, NI), jax.random.fold_in(key_list[2], 1), 0, NI - 1).astype(jnp.int32)
    leaf_factor = draw_leaf_factor(jax.random.fold_in(key_list[11], 71), 0)
    coupling1 = centred(key_list[4], (DEVICES * NI, NS1), (4 * NI) ** -0.5, 0.0625, ((0, 128),))
    coupling2 = centred(key_list[5], (DEVICES * NI, NS2), (4 * NI) ** -0.5, 0.0625, ((0, 128),))
    sep_coupling = centred(key_list[6], (N_BX * NS1, NS2), NS1 ** -0.5, 0.25, ((0, 128),))
    sep1_factor = draw_sep1_factor(jax.random.fold_in(key_list[11], 71), 0)
    sep2_factor = draw_sep2_factor(jax.random.fold_in(key_list[11], 71), 0)
    sep1_rhs = centred(key_list[9], (R, N_BX * NS1), 1.0, 6.0, ((1, 128),), jnp.float32)
    sep2_rhs = centred(key_list[10], (R, NS2), 1.0, 6.0, ((1, 128),), jnp.float32)
    return {"sensitivities": sensitivities, "owner": owner, "owner_cell": owner_cell, "leaf_factor": leaf_factor, "coupling1": coupling1, "coupling2": coupling2, "sep_coupling": sep_coupling, "sep1_factor": sep1_factor, "sep2_factor": sep2_factor, "sep1_rhs": sep1_rhs, "sep2_rhs": sep2_rhs}


def reference(sensitivities, owner, owner_cell, leaf_factor, coupling1, coupling2, sep_coupling, sep1_factor, sep2_factor, sep1_rhs, sep2_rhs):
    bf = jnp.bfloat16
    f32 = jnp.float32
    target = (owner[:, 0] * NI + owner_cell).astype(jnp.int32)
    load = jnp.zeros((R, DEVICES * NI), f32).at[:, target].add(sensitivities)
    load = load.reshape(R, DEVICES, NI).transpose(1, 0, 2)
    coupling1_d = coupling1.reshape(DEVICES, NI, NS1)
    coupling2_d = coupling2.reshape(DEVICES, NI, NS2)
    leaf_y = lax.map(lambda a: jnp.dot(a[0].astype(bf), a[1], preferred_element_type=f32), (load, leaf_factor))
    leaf_yb = leaf_y.astype(bf)
    upd1 = lax.map(lambda a: jnp.dot(a[0], a[1], preferred_element_type=f32), (leaf_yb, coupling1_d))
    z1 = sep1_rhs.reshape(R, N_BX, NS1).transpose(1, 0, 2) - jnp.sum(upd1.reshape(N_BX, N_BY, R, NS1), axis=1)
    sep1_mat = sep1_factor.reshape(N_BX, NS1, NS1).astype(f32)
    sep_mat = sep_coupling.reshape(N_BX, NS1, NS2).astype(f32)
    sep1_y = jnp.einsum("irk,isk->irs", z1.astype(bf).astype(f32), sep1_mat)
    upd2 = lax.map(lambda a: jnp.dot(a[0], a[1], preferred_element_type=f32), (leaf_yb, coupling2_d))
    upd_sep = jnp.einsum("irk,iks->rs", sep1_y.astype(bf).astype(f32), sep_mat)
    z2 = sep2_rhs - jnp.sum(upd2, axis=0) - upd_sep
    sep2_y = lax.dot_general(z2.astype(bf), sep2_factor, (((1,), (1,)), ((), ())), preferred_element_type=f32)
    sep2_field = jnp.dot(sep2_y.astype(bf), sep2_factor, preferred_element_type=f32)
    sep2_b = sep2_field.astype(bf)
    back1 = sep1_y - jnp.einsum("rs,iks->irk", sep2_b.astype(f32), sep_mat)
    sep1_out = jnp.einsum("irk,iks->irs", back1.astype(bf).astype(f32), sep1_mat)
    sep1_b = jnp.repeat(sep1_out.astype(bf), N_BY, axis=0)

    def leaf_back(a):
        y_d, s1, c1, c2, g_d = a
        rest = y_d - lax.dot_general(s1, c1, (((1,), (1,)), ((), ())), preferred_element_type=f32)
        rest = rest - lax.dot_general(sep2_b, c2, (((1,), (1,)), ((), ())), preferred_element_type=f32)
        return lax.dot_general(rest.astype(bf), g_d, (((1,), (1,)), ((), ())), preferred_element_type=f32)

    filtered = lax.map(leaf_back, (leaf_y, sep1_b, coupling1_d, coupling2_d, leaf_factor))
    filtered = filtered.transpose(1, 0, 2).reshape(R, DEVICES * NI)
    sep1_field = sep1_out.transpose(1, 0, 2).reshape(R, N_BX * NS1)
    return filtered, sep1_field, sep2_field
```

```python
import functools

import jax
import jax.numpy as jnp
from jax import lax
from jax.experimental import pallas as pl
from jax.experimental.pallas import tpu as pltpu
from jax.sharding import PartitionSpec as P

BF = jnp.bfloat16
F32 = jnp.float32
I32 = jnp.int32
MESH = pl.DeviceIdType.MESH
GROUPS = 4
SLOTS = 128
CHUNK = 256
WIDE = 1024


def nn(a, b):
    return jnp.dot(a, b, preferred_element_type=F32)


def nt(a, b):
    return lax.dot_general(a, b, (((1,), (1,)), ((), ())), preferred_element_type=F32)


def hot(mask, like=BF):
    return jnp.where(mask, 1.0, 0.0).astype(like)


def kernel(
    nbx, nby,
    sens, owner, cell, g_h, c_h, e_h, f_h, v1_h, v2, rhs1, rhs2,
    filt, s1o, s2o,
    g, c, e, f, v1, lt, hb, vb, a, acc, acc3, base, packed, pcell, recv, rcell,
    ly, v2g, pad, p1, p2, ex1, ex3s, ex3, ex4, ex5, ex6s, ex6, ex7, ex8,
    load_sem, send_v, send_c, recv_v, recv_c, ssem, rsem,
):
    nd = nbx * nby
    gs = nd // GROUPS
    hg = gs // 2
    nh = nd // 2
    rr, held = sens.shape
    bx = lax.axis_index("bx")
    by = lax.axis_index("by")
    me = bx * nby + by
    mine = lax.rem(me, gs)
    mygroup = me // gs

    loads = []
    for k, (src, dst) in enumerate(((g_h, g), (c_h, c), (e_h, e), (f_h, f), (v1_h, v1))):
        cp = pltpu.make_async_copy(src, dst, load_sem.at[k])
        cp.start()
        loads.append(cp)

    barrier = pltpu.get_barrier_semaphore()

    def greet(k, _):
        @pl.when(k != me)
        def _():
            pl.semaphore_signal(
                barrier, inc=1, device_id=(k // nby, lax.rem(k, nby)), device_id_type=MESH
            )
        return 0

    lax.fori_loop(0, nd, greet, 0)

    base[...] = jnp.zeros_like(base)
    acc3[...] = jnp.zeros_like(acc3)

    def rank_step(k, _):
        ks = pl.ds(pl.multiple_of(k * CHUNK, CHUNK), CHUNK)
        own = owner[:, ks]
        dtf = jnp.where(lax.broadcasted_iota(I32, (nd, CHUNK), 0) == own, 1.0, 0.0)
        dtb = dtf.astype(BF)
        up = hot(
            lax.broadcasted_iota(I32, (CHUNK, CHUNK), 0)
            < lax.broadcasted_iota(I32, (CHUNK, CHUNK), 1)
        )
        pre = nn(dtb, up)
        tot = nn(dtb, jnp.ones((CHUNK, 128), BF))
        b = base[...]
        pos = jnp.sum((pre + jnp.concatenate([b, b], axis=1)) * dtf, axis=0, keepdims=True)
        base[...] = b + tot
        slot = pos.astype(I32) + SLOTS * (own & 1)
        ltc = hot(lax.broadcasted_iota(I32, (2 * SLOTS, CHUNK), 0) == slot)
        lt[:, ks] = ltc
        hv = own >> 1
        hb[:, ks] = jnp.broadcast_to(hv.astype(F32), (16, CHUNK)).astype(BF)
        vb[:, ks] = sens[:, ks].astype(BF)
        ce = cell[:, ks]
        m = lax.broadcasted_iota(I32, (nh, CHUNK), 0) == hv
        hi = jnp.where(m, (ce >> 8).astype(F32), 0.0)
        lo = jnp.where(m, (ce & 255).astype(F32), 0.0)
        acc3[...] += nt(jnp.concatenate([hi, lo], axis=0).astype(BF), ltc)
        return 0

    lax.fori_loop(0, held // CHUNK, rank_step, 0)
    cells = acc3[0:nh, :] * 256.0 + acc3[nh : 2 * nh, :]
    for h in range(nh):
        for half in range(2):
            pcell[2 * h + half] = cells[h : h + 1, half * SLOTS : (half + 1) * SLOTS]

    rows2 = v2.shape[0]
    v2at = pl.ds(pl.multiple_of(bx * rows2, rows2), rows2)
    v2g[v2at, :] = v2[...].astype(F32)

    pl.semaphore_wait(barrier, nd - 1)

    for r in range(1, nbx):
        pltpu.make_async_remote_copy(
            v2g.at[v2at], v2g.at[v2at], ssem.at[0], rsem.at[0],
            device_id=(lax.rem(bx + r, nbx), by), device_id_type=MESH,
        ).start()

    def group_step(t, _):
        gi = lax.rem(t + 2, GROUPS)
        there = lax.rem(mygroup + gi, GROUPS)
        first = there * hg
        acc[...] = jnp.zeros_like(acc)

        def pack_step(k, _):
            ks = pl.ds(pl.multiple_of(k * WIDE, WIDE), WIDE)
            hk = hb[:, ks]
            for h in range(hg):
                m = hk == (first + h).astype(F32).astype(BF)
                for q in range(rr // 16):
                    rows = slice(h * rr + q * 16, h * rr + q * 16 + 16)
                    a[rows, :] = jnp.where(m, vb[q * 16 : q * 16 + 16, ks], jnp.zeros((), BF))
            acc[0 : hg * rr, :] += nt(a[0 : hg * rr, :], lt[:, ks])
            return 0

        lax.fori_loop(0, held // WIDE, pack_step, 0)
        for h in range(hg):
            for half in range(2):
                packed[gi, 2 * h + half] = acc[
                    h * rr : (h + 1) * rr, half * SLOTS : (half + 1) * SLOTS
                ].astype(BF)

        def send_step(s, _):
            d = there * gs + s

            @pl.when(d != me)
            def _():
                to = (d // nby, lax.rem(d, nby))
                pltpu.make_async_remote_copy(
                    packed.at[gi, s], recv.at[gi, mine], send_v.at[gi], recv_v.at[gi],
                    device_id=to, device_id_type=MESH,
                ).start()
                pltpu.make_async_remote_copy(
                    pcell.at[d], rcell.at[gi, mine], send_c.at[gi], recv_c.at[gi],
                    device_id=to, device_id_type=MESH,
                ).start()
            return 0

        lax.fori_loop(0, gs, send_step, 0)
        return 0

    lax.fori_loop(0, GROUPS, group_step, 0)
    recv[0, mine] = packed[0, mine]
    rcell[0, mine] = pcell[me]

    step = WIDE // SLOTS
    ncell = 2048 // 256
    pieces = min(step, gs)
    acc[0:256, :] = jnp.zeros((256, 256), F32)
    for t in range(GROUPS):
        gi = (t + 2) % GROUPS
        n = gs - 1 if gi == 0 else gs
        got = recv.at[gi, pl.ds(0, n)]
        pltpu.make_async_copy(got, got, recv_v.at[gi]).wait()
        got = rcell.at[gi, pl.ds(0, n)]
        pltpu.make_async_copy(got, got, recv_c.at[gi]).wait()

        def land_step(s, _):
            hots = []
            for p in range(pieces):
                ci = rcell[gi, s * pieces + p].astype(I32)
                hots.append(hot(lax.broadcasted_iota(I32, (256, SLOTS), 0) == (ci & 255)))
                chb = jnp.broadcast_to((ci >> 8).astype(F32), (16, SLOTS)).astype(BF)
                lanes = slice(p * SLOTS, (p + 1) * SLOTS)
                blk = recv[gi, s * pieces + p]
                for ch in range(ncell):
                    m = chb == jnp.asarray(ch, BF)
                    for q in range(rr // 16):
                        rows = slice(ch * rr + q * 16, ch * rr + q * 16 + 16)
                        a[rows, lanes] = jnp.where(
                            m, blk[q * 16 : q * 16 + 16, :], jnp.zeros((), BF)
                        )
            acc[0:256, :] += nt(
                a[0:256, 0 : pieces * SLOTS], jnp.concatenate(hots, axis=1)
            )
            return 0

        lax.fori_loop(0, gs // pieces, land_step, 0)

    load = jnp.concatenate(
        [acc[ch * rr : (ch + 1) * rr, :].astype(BF) for ch in range(ncell)], axis=1
    )

    for cp in loads:
        cp.wait()
    ni = g.shape[0]
    for n in range(ni // 512):
        cols = slice(n * 512, (n + 1) * 512)
        ly[:, cols] = nn(load, g[:, cols])
    lyb = ly[...].astype(BF)

    def placed(part, rhs, share, index):
        per = 128 // share
        pad[...] = jnp.zeros_like(pad)
        pad[:, 0:share] = rhs[...]
        turned = pltpu.roll(pad[...], lax.rem(index, per) * share, 1)
        at = pl.ds(pl.multiple_of((index // per) * 128, 128), 128)
        part[:, at] = part[:, at] + turned

    def spread(k, src_of, dst):
        for r in range(1, nby):
            j = lax.rem(by + r, nby)
            pltpu.make_async_remote_copy(
                src_of(j), dst, ssem.at[k], rsem.at[k],
                device_id=(bx, j), device_id_type=MESH,
            ).start()

    def arrived(k, buf, n):
        got = buf.at[pl.ds(0, n)]
        pltpu.make_async_copy(got, got, rsem.at[k]).wait()

    def left(k, buf, n):
        got = buf.at[pl.ds(0, n)]
        pltpu.make_async_copy(got, got, ssem.at[k]).wait()

    def total(buf):
        out = buf[0].astype(F32)
        for j in range(1, buf.shape[0]):
            out = out + buf[j].astype(F32)
        return out

    p1[...] = -nn(lyb, c[...])
    placed(p1, rhs1, rhs1.shape[1], by)
    ex1[by] = p1[...].astype(BF)
    spread(1, lambda j: ex1.at[by], ex1.at[by])
    p2[...] = -nn(lyb, e[...])
    placed(p2, rhs2, rhs2.shape[1], me)
    arrived(1, ex1, nby - 1)
    z1b = total(ex1).astype(BF)
    s1y = nt(z1b, v1[...])
    part2 = p2[...] - nn(s1y.astype(BF), f[...])
    for j in range(nby):
        ex3s[j] = part2[:, j * 128 : (j + 1) * 128].astype(BF)
    spread(2, lambda j: ex3s.at[j], ex3.at[by])
    ex3[by] = ex3s[by]
    arrived(0, v2g, (nbx - 1) * rows2)
    v2r = v2g[...].astype(BF)
    arrived(2, ex3, nby - 1)
    ex4[bx] = total(ex3).astype(BF)
    for r in range(1, nbx):
        pltpu.make_async_remote_copy(
            ex4.at[bx], ex4.at[bx], ssem.at[3], rsem.at[3],
            device_id=(lax.rem(bx + r, nbx), by), device_id_type=MESH,
        ).start()
    arrived(3, ex4, nbx - 1)
    ex5[by] = total(ex4).astype(BF)
    spread(4, lambda j: ex5.at[by], ex5.at[by])
    arrived(4, ex5, nby - 1)
    z2b = jnp.concatenate([ex5[j] for j in range(nby)], axis=1)

    y2 = nt(z2b, v2r).astype(BF)
    part = nn(y2, v2r)
    for j in range(nby):
        ex6s[j] = part[:, j * 128 : (j + 1) * 128].astype(BF)
    spread(5, lambda j: ex6s.at[j], ex6.at[by])
    ex6[by] = ex6s[by]
    arrived(5, ex6, nby - 1)
    ex7[by] = total(ex6)
    spread(6, lambda j: ex7.at[by], ex7.at[by])
    arrived(6, ex7, nby - 1)
    s2 = jnp.concatenate([ex7[j] for j in range(nby)], axis=1)
    s2o[...] = s2
    s2b = s2.astype(BF)

    back1 = s1y - nt(s2b, f[...])
    ex8[by] = nn(back1.astype(BF), v1[...]).astype(BF)
    spread(7, lambda j: ex8.at[by], ex8.at[by])
    for n in range(ni // 512):
        cols = slice(n * 512, (n + 1) * 512)
        ly[:, cols] = ly[:, cols] - nt(s2b, e[cols, :])
    arrived(7, ex8, nby - 1)
    s1 = total(ex8)
    s1o[...] = s1
    s1b = s1.astype(BF)
    for n in range(ni // 512):
        cols = slice(n * 512, (n + 1) * 512)
        ly[:, cols] = ly[:, cols] - nt(s1b, c[cols, :])
    rest = ly[...].astype(BF)
    for n in range(ni // 512):
        cols = slice(n * 512, (n + 1) * 512)
        filt[:, cols] = nt(rest, g[cols, :])

    left(0, v2g, (nbx - 1) * rows2)
    left(1, ex1, nby - 1)
    left(2, ex3, nby - 1)
    left(3, ex4, nbx - 1)
    left(4, ex5, nby - 1)
    left(5, ex6, nby - 1)
    left(6, ex7, nby - 1)
    left(7, ex8, nby - 1)
    for gi in range(GROUPS):
        n = gs - 1 if gi == 0 else gs
        got = packed.at[gi, pl.ds(0, n)]
        pltpu.make_async_copy(got, got, send_v.at[gi]).wait()
        got = rcell.at[gi, pl.ds(0, n)]
        pltpu.make_async_copy(got, got, send_c.at[gi]).wait()


def body(nbx, nby, sens, owner, cell, g, c, e, f, v1, v2, rhs1, rhs2):
    nd = nbx * nby
    gs = nd // GROUPS
    rr, held = sens.shape
    ni = g.shape[1]
    ns1 = c.shape[1]
    ns2 = e.shape[1]
    vmem = pl.BlockSpec(memory_space=pltpu.VMEM)
    hbm = pl.BlockSpec(memory_space=pl.ANY)
    rows = max(gs // 2 * rr, 256)
    scratch = [
        pltpu.VMEM((ni, ni), BF),
        pltpu.VMEM((ni, ns1), BF),
        pltpu.VMEM((ni, ns2), BF),
        pltpu.VMEM(f.shape, BF),
        pltpu.VMEM(v1.shape, BF),
        pltpu.VMEM((2 * SLOTS, held), BF),
        pltpu.VMEM((16, held), BF),
        pltpu.VMEM((rr, held), BF),
        pltpu.VMEM((rows, WIDE), BF),
        pltpu.VMEM((rows, 256), F32),
        pltpu.VMEM((nd, 256), F32),
        pltpu.VMEM((nd, 128), F32),
        pltpu.VMEM((GROUPS, gs, rr, SLOTS), BF),
        pltpu.VMEM((nd, 1, SLOTS), F32),
        pltpu.VMEM((GROUPS, gs, rr, SLOTS), BF),
        pltpu.VMEM((GROUPS, gs, 1, SLOTS), F32),
        pltpu.VMEM((rr, ni), F32),
        pltpu.VMEM((v2.shape[0] * nbx, ns2), F32),
        pltpu.VMEM((rr, 128), F32),
        pltpu.VMEM((rr, ns1), F32),
        pltpu.VMEM((rr, ns2), F32),
        pltpu.VMEM((nby, rr, ns1), BF),
        pltpu.VMEM((nby, rr, 128), BF),
        pltpu.VMEM((nby, rr, 128), BF),
        pltpu.VMEM((nbx, rr, 128), BF),
        pltpu.VMEM((nby, rr, 128), BF),
        pltpu.VMEM((nby, rr, 128), BF),
        pltpu.VMEM((nby, rr, 128), BF),
        pltpu.VMEM((nby, rr, 128), F32),
        pltpu.VMEM((nby, rr, ns1), BF),
        pltpu.SemaphoreType.DMA((5,)),
        pltpu.SemaphoreType.DMA((GROUPS,)),
        pltpu.SemaphoreType.DMA((GROUPS,)),
        pltpu.SemaphoreType.DMA((GROUPS,)),
        pltpu.SemaphoreType.DMA((GROUPS,)),
        pltpu.SemaphoreType.DMA((8,)),
        pltpu.SemaphoreType.DMA((8,)),
    ]
    return pl.pallas_call(
        functools.partial(kernel, nbx, nby),
        out_shape=(
            jax.ShapeDtypeStruct((rr, ni), F32),
            jax.ShapeDtypeStruct((rr, ns1), F32),
            jax.ShapeDtypeStruct((rr, ns2), F32),
        ),
        in_specs=[vmem] * 3 + [hbm] * 5 + [vmem] * 3,
        out_specs=(vmem,) * 3,
        scratch_shapes=scratch,
        compiler_params=pltpu.CompilerParams(
            collective_id=0, has_side_effects=True, vmem_limit_bytes=48 << 20
        ),
    )(
        sens, owner.reshape(1, held), cell.reshape(1, held), g.reshape(ni, ni),
        c, e, f, v1, v2, rhs1, rhs2,
    )


def solution(mesh):
    nbx, nby = mesh.shape["bx"], mesh.shape["by"]
    both = ("bx", "by")
    in_specs = (
        P(None, both), P(both, None), P(both), P(both, None, None),
        P(both, None), P(both, None), P(both, None), P(both, None), P(both, None),
        P(None, both), P(None, both),
    )
    out_specs = (P(None, both), P(None, "bx"), P())
    return jax.shard_map(
        functools.partial(body, nbx, nby), mesh=mesh, in_specs=in_specs, out_specs=out_specs,
        check_vma=False,
    )
```

```python
import functools

import jax
import jax.numpy as jnp
from jax import lax
from jax.experimental import pallas as pl
from jax.experimental.pallas import tpu as pltpu
from jax.sharding import PartitionSpec as P

BF = jnp.bfloat16
F32 = jnp.float32
I32 = jnp.int32
MESH = pl.DeviceIdType.MESH
SLOTS = 128
CHUNK = 256
WIDE = 2048
LAND = 1024


def nn(a, b):
    return jnp.dot(a, b, preferred_element_type=F32)


def nt(a, b):
    return lax.dot_general(a, b, (((1,), (1,)), ((), ())), preferred_element_type=F32)


def hot(mask):
    return jnp.where(mask, jnp.ones((), BF), jnp.zeros((), BF))


def rows16(row, count=16):
    return jnp.broadcast_to(row.astype(F32), (count, row.shape[1])).astype(BF)


def kernel(
    nbx, nby,
    sens_h, owner_h, cell_h, g_h, c_h, e_h, f_h, v1_h, v2_h, rhs1_h, rhs2_h,
    filt, s1o, s2o,
    sens, owner, cell, g, c, e, ff, vv, v2s, rhs1, rhs2,
    io, up, lt, hb, vb, a, cl, acc, acc3, base, packed, pcell, recv, rcell,
    ly, v2x, v2f, pad, p1, p2, ex1, ex3s, ex3, ex4, ex5,
    load_sem, send_v, send_c, recv_v, recv_c, ssem, rsem,
):
    nx = 4 if nbx == 16 else 2
    ny = nbx // nx
    nz = nby // 2
    nd = nbx * nby
    gs = nd // nx
    hg = gs // 2
    nh = nd // 2
    rr, held = sens.shape
    bx = lax.axis_index("bx")
    by = lax.axis_index("by")
    me = bx * nby + by
    mine = lax.rem(me, gs)
    mygroup = me // gs
    x, y = bx // ny, lax.rem(bx, ny)
    z, core = by // 2, lax.rem(by, 2)
    outer = x * (1 - core) + y * core
    inner = y * (1 - core) + x * core

    def bx_of(far, near):
        return far * (ny * (1 - core) + core) + near * ((1 - core) + ny * core)

    loads = []
    pairs = (
        (owner_h, owner), (cell_h, cell), (sens_h, sens), (v2_h, v2s),
        (f_h, ff.at[core, z]), (v1_h, vv.at[core, z]), (rhs1_h, rhs1), (rhs2_h, rhs2),
        (c_h, c), (e_h, e), (g_h, g),
    )
    for k, (src, dst) in enumerate(pairs):
        cp = pltpu.make_async_copy(src, dst, load_sem.at[k])
        cp.start()
        loads.append(cp)

    barrier = pltpu.get_barrier_semaphore()

    def greet(k, _):
        d = lax.rem(me + k, nd)
        pl.semaphore_signal(
            barrier, inc=1, device_id=(d // nby, lax.rem(d, nby)), device_id_type=MESH
        )
        return 0

    lax.fori_loop(1, nd, greet, 0)

    io[...] = lax.broadcasted_iota(I32, (256, 128), 0).astype(F32).astype(BF)
    up[:, 0:CHUNK] = jnp.where(
        lax.broadcasted_iota(I32, (CHUNK, CHUNK), 0)
        < lax.broadcasted_iota(I32, (CHUNK, CHUNK), 1),
        1.0, 0.0,
    ).astype(BF)
    up[:, CHUNK:] = jnp.ones((CHUNK, 128), BF)

    def counting(first, count, lanes):
        block = io[first : first + count, :]
        return jnp.concatenate([block] * (lanes // 128), axis=1)

    base[...] = jnp.zeros_like(base)
    acc3[...] = jnp.zeros_like(acc3)
    for cp in loads[0:3]:
        cp.wait()
    nb = min(16, nh)

    def rank_chunk(ks):
        own = owner[:, ks]
        ob = rows16(own)
        dtb = jnp.concatenate(
            [hot(counting(i, min(16, nd), CHUNK) == ob[0 : min(16, nd)]) for i in range(0, nd, 16)],
            axis=0,
        )
        pre = nn(dtb, up[...])
        b = base[...]
        m = lax.broadcasted_iota(I32, (nd, CHUNK), 0) == own
        ranked = pre[:, 0:CHUNK] + jnp.concatenate([b, b], axis=1)
        pos = jnp.sum(jnp.where(m, ranked, 0.0), axis=0, keepdims=True)
        base[...] = b + pre[:, CHUNK:]
        sb = rows16(pos + (SLOTS * (own & 1)).astype(F32))
        for i in range(0, 2 * SLOTS, 16):
            lt[i : i + 16, ks] = hot(counting(i, 16, CHUNK) == sb)
        hk = rows16(own >> 1)
        hb[:, ks] = hk
        vb[:, ks] = sens[:, ks].astype(BF)
        ce = cell[:, ks]
        hi = rows16(ce >> 8)
        lo = rows16(ce & 255)
        ms = [counting(i, nb, CHUNK) == hk[0:nb] for i in range(0, nh, nb)]
        a3 = [jnp.where(m3, w[0:nb], jnp.zeros((), BF)) for w in (hi, lo) for m3 in ms]
        return jnp.concatenate(a3, axis=0)

    def rank_step(k, _):
        a3 = []
        for q in range(4):
            a3.append(rank_chunk(pl.ds(pl.multiple_of((k * 4 + q) * CHUNK, CHUNK), CHUNK)))
        ks = pl.ds(pl.multiple_of(k * 4 * CHUNK, 4 * CHUNK), 4 * CHUNK)
        acc3[...] += nt(jnp.concatenate(a3, axis=1), lt[:, ks])
        return 0

    rank_steps = held // (4 * CHUNK)
    lax.fori_loop(0, min(2, rank_steps), rank_step, 0)

    for cp in loads[3:6]:
        cp.wait()
    r2 = v2s.shape[0]
    half2 = v2s.shape[1] // 2
    v2v = v2s[...].astype(F32)
    v2x[core, outer, inner, z] = jnp.concatenate(
        [v2v[:, 0:half2], v2v[:, half2:]], axis=0
    ).astype(BF)

    def remote(src, dst, k, where):
        pltpu.make_async_remote_copy(
            src, dst, ssem.at[k], rsem.at[k], device_id=where, device_id_type=MESH
        ).start()

    def came(k, ref):
        pltpu.make_async_copy(ref, ref, rsem.at[k]).wait()

    def went(k, ref):
        pltpu.make_async_copy(ref, ref, ssem.at[k]).wait()

    pl.semaphore_wait(barrier, nd - 1)

    stage_z = (v2x.at[core, outer, inner], ff.at[core], vv.at[core])

    def gather_z():
        for r in range(1, nz):
            to = (bx, lax.rem(z + r, nz) * 2 + core)
            for k, buf in enumerate(stage_z):
                remote(buf.at[z], buf.at[z], k, to)

    def gather_inner():
        if nz > 1:
            came(0, stage_z[0].at[pl.ds(0, nz - 1)])
        blk = v2x.at[core, outer, inner]
        for r in range(1, ny):
            remote(blk, blk, 3, (bx_of(outer, lax.rem(inner + r, ny)), by))

    def gather_outer():
        came(3, v2x.at[core, outer, pl.ds(0, ny - 1)])
        blk = v2x.at[core, outer]
        for r in range(1, nx):
            remote(blk, blk, 4, (bx_of(lax.rem(outer + r, nx), inner), by))

    partner = (bx, z * 2 + 1 - core)

    def gather_pair():
        if nz > 1:
            came(1, ff.at[core, pl.ds(0, nz - 1)])
            came(2, vv.at[core, pl.ds(0, nz - 1)])
        for k, buf in ((5, ff), (6, vv)):
            remote(buf.at[core], buf.at[core], k, partner)

    def gather_top():
        came(4, v2x.at[core, pl.ds(0, nx - 1)])
        remote(v2x.at[core], v2x.at[core], 7, partner)

    gather_z()
    lax.fori_loop(min(2, rank_steps), rank_steps, rank_step, 0)
    cells = acc3[0:nh, :] * 256.0 + acc3[nh : 2 * nh, :]
    for h in range(nh):
        for half in range(2):
            pcell[2 * h + half] = cells[h : h + 1, half * SLOTS : (half + 1) * SLOTS]

    order = [2, 1, 3, 0] if nx == 4 else [1, 0]
    steps = held // WIDE if held >= WIDE else 1
    wide = held // steps
    per = gs // steps

    def send(gi, s):
        t = lax.rem(mine + s, gs)
        d = lax.rem(mygroup + gi, nx) * gs + t
        to = (d // nby, lax.rem(d, nby))
        pltpu.make_async_remote_copy(
            packed.at[gi, t], recv.at[gi, mine], send_v.at[gi], recv_v.at[gi],
            device_id=to, device_id_type=MESH,
        ).start()
        pltpu.make_async_remote_copy(
            pcell.at[d], rcell.at[gi, mine], send_c.at[gi], recv_c.at[gi],
            device_id=to, device_id_type=MESH,
        ).start()

    def pack(gi, before):
        first = lax.rem(mygroup + gi, nx) * hg
        acc[...] = jnp.zeros_like(acc)

        def pack_step(k, _):
            ks = pl.ds(pl.multiple_of(k * wide, wide), wide)
            if before is not None:
                for q in range(per):
                    send(before, k * per + q)
            hk = hb[:, ks]
            for h in range(hg):
                m = hk == (first + h).astype(F32).astype(BF)
                for q in range(rr // 16):
                    rows = slice(h * rr + q * 16, h * rr + q * 16 + 16)
                    a[rows, 0:wide] = jnp.where(
                        m, vb[q * 16 : q * 16 + 16, ks], jnp.zeros((), BF)
                    )
            acc[0 : hg * rr, :] += nt(a[0 : hg * rr, 0:wide], lt[:, ks])
            return 0

        lax.fori_loop(0, steps, pack_step, 0)
        for h in range(hg):
            for half in range(2):
                packed[gi, 2 * h + half] = acc[
                    h * rr : (h + 1) * rr, half * SLOTS : (half + 1) * SLOTS
                ].astype(BF)

    gather_inner()
    for t, gi in enumerate(order):
        pack(gi, order[t - 1] if t else None)

    def last_step(s, _):
        send(0, s)
        return 0

    lax.fori_loop(1, gs, last_step, 0)
    gather_outer()
    recv[0, mine] = packed[0, mine]
    rcell[0, mine] = pcell[me]

    ncell = 2048 // 256
    pieces = min(LAND // SLOTS, gs)
    acc[0:256, :] = jnp.zeros((256, 256), F32)

    def land(gi):
        n = gs - 1 if gi == 0 else gs
        got = recv.at[gi, pl.ds(0, n)]
        pltpu.make_async_copy(got, got, recv_v.at[gi]).wait()
        got = rcell.at[gi, pl.ds(0, n)]
        pltpu.make_async_copy(got, got, recv_c.at[gi]).wait()

        def land_step(s, _):
            for p in range(pieces):
                ci = rcell[gi, s * pieces + p].astype(I32)
                lanes = slice(p * SLOTS, (p + 1) * SLOTS)
                lob = rows16(ci & 255)
                hib = rows16(ci >> 8)
                for i in range(0, 256, 16):
                    cl[i : i + 16, lanes] = hot(io[i : i + 16, :] == lob)
                blk = recv[gi, s * pieces + p]
                for ch in range(ncell):
                    m = hib == jnp.asarray(ch, BF)
                    for q in range(rr // 16):
                        rows = slice(ch * rr + q * 16, ch * rr + q * 16 + 16)
                        a[rows, lanes] = jnp.where(
                            m, blk[q * 16 : q * 16 + 16, :], jnp.zeros((), BF)
                        )
            wide_k = slice(0, pieces * SLOTS)
            acc[0:256, :] += nt(a[0:256, wide_k], cl[:, wide_k])
            return 0

        lax.fori_loop(0, gs // pieces, land_step, 0)

    for gi in order:
        land(gi)

    gather_pair()
    load = jnp.concatenate(
        [acc[ch * rr : (ch + 1) * rr, :].astype(BF) for ch in range(ncell)], axis=1
    )

    for cp in loads[6:]:
        cp.wait()
    ni = g.shape[0]
    tiles = [slice(n, n + 512) for n in range(0, ni, 512)]
    for cols in tiles:
        ly[:, cols] = nn(load, g[:, cols])
    lyb = ly[...].astype(BF)

    def placed(part, rhs, share, index):
        per_block = 128 // share
        turned = pltpu.roll(rhs, lax.rem(index, per_block) * share, 1)
        at = pl.ds(pl.multiple_of((index // per_block) * 128, 128), 128)
        part[:, at] = part[:, at] + turned

    def spread(k, src_of, dst):
        for r in range(1, nby):
            j = lax.rem(by + r, nby)
            remote(src_of(j), dst, k, (bx, j))

    def total(buf):
        out = buf[0].astype(F32)
        for j in range(1, buf.shape[0]):
            out = out + buf[j].astype(F32)
        return out

    p1[...] = -nn(lyb, c[...])
    pad[...] = jnp.zeros_like(pad)
    pad[0:rr, 0 : rhs1.shape[1]] = rhs1[...]
    placed(p1, pad[0:rr, :], rhs1.shape[1], by)
    ex1[by] = p1[...].astype(BF)
    u = ex1[by]
    p2[...] = -nn(lyb, e[...])
    pad[...] = jnp.zeros_like(pad)
    pad[0 : rhs2.shape[0], 0:rr] = rhs2[...]
    placed(p2, pad[...].T[0:rr, :], rhs2.shape[0], me)

    came(5, ff.at[core])
    came(6, vv.at[core])
    ns1, ns2 = p1.shape[1], p2.shape[1]
    v1 = vv[...].reshape(ns1, ns1)
    f = ff[...].reshape(ns1, ns2)
    part2 = p2[...] - nn(nt(u, v1).astype(BF), f)
    for j in range(nby):
        ex3s[j] = part2[:, j * 128 : (j + 1) * 128].astype(BF)
    spread(9, lambda j: ex3s.at[j], ex3.at[by])
    spread(8, lambda j: ex1.at[by], ex1.at[by])
    ex3[by] = ex3s[by]
    gather_top()

    came(9, ex3.at[pl.ds(0, nby - 1)])
    ex4[bx] = total(ex3).astype(BF)
    for r in range(1, nbx):
        remote(ex4.at[bx], ex4.at[bx], 10, (lax.rem(bx + r, nbx), by))
    came(8, ex1.at[pl.ds(0, nby - 1)])
    s1y = nt(total(ex1).astype(BF), v1)
    came(7, v2x.at[core])
    some = ny * nz

    def turn_step(k, _):
        blocks = v2x[k // nx, lax.rem(k, nx)].astype(F32).reshape(some, 2 * r2, half2)
        at = pl.ds(pl.multiple_of(k * some * r2, some * r2), some * r2)
        v2f[at, 0:half2] = blocks[:, 0:r2].reshape(some * r2, half2).astype(BF)
        v2f[at, half2:] = blocks[:, r2:].reshape(some * r2, half2).astype(BF)
        return 0

    lax.fori_loop(0, 2 * nx, turn_step, 0)

    came(10, ex4.at[pl.ds(0, nbx - 1)])
    ex5[by] = total(ex4).astype(BF)
    spread(11, lambda j: ex5.at[by], ex5.at[by])
    came(11, ex5.at[pl.ds(0, nby - 1)])
    z2b = jnp.concatenate([ex5[j] for j in range(nby)], axis=1)

    y2 = nt(z2b, v2f[...]).astype(BF)
    s2 = nn(y2, v2f[...])
    s2o[...] = s2
    s2b = s2.astype(BF)
    back1 = s1y - nt(s2b, f)
    s1 = nn(back1.astype(BF), v1)
    s1o[...] = s1
    s1b = s1.astype(BF)
    for cols in tiles:
        ly[:, cols] = ly[:, cols] - nt(s1b, c[cols, :]) - nt(s2b, e[cols, :])
    rest = ly[...].astype(BF)
    for cols in tiles:
        filt[:, cols] = nt(rest, g[cols, :])

    if nz > 1:
        for k, buf in enumerate(stage_z):
            went(k, buf.at[pl.ds(0, nz - 1)])
    went(3, v2x.at[core, outer, pl.ds(0, ny - 1)])
    went(4, v2x.at[core, pl.ds(0, nx - 1)])
    for k, buf in ((5, ff), (6, vv), (7, v2x)):
        went(k, buf.at[core])
    went(8, ex1.at[pl.ds(0, nby - 1)])
    went(9, ex3.at[pl.ds(0, nby - 1)])
    went(10, ex4.at[pl.ds(0, nbx - 1)])
    went(11, ex5.at[pl.ds(0, nby - 1)])
    for gi in range(nx):
        n = gs - 1 if gi == 0 else gs
        got = packed.at[gi, pl.ds(0, n)]
        pltpu.make_async_copy(got, got, send_v.at[gi]).wait()
        got = rcell.at[gi, pl.ds(0, n)]
        pltpu.make_async_copy(got, got, send_c.at[gi]).wait()


def store(filt, s1, s2, filt_h, s1_h, s2_h, sem):
    copies = [
        pltpu.make_async_copy(src, dst, sem.at[k])
        for k, (src, dst) in enumerate(((filt, filt_h), (s1, s1_h), (s2, s2_h)))
    ]
    for cp in copies:
        cp.start()
    for cp in copies:
        cp.wait()


def body(nbx, nby, sens, owner, cell, g, c, e, f, v1, v2, rhs1, rhs2):
    nx = 4 if nbx == 16 else 2
    ny, nz = nbx // nx, nby // 2
    nd = nbx * nby
    gs = nd // nx
    rr, held = sens.shape
    ni = g.shape[1]
    ns1 = c.shape[1]
    ns2 = e.shape[1]
    vmem = pl.BlockSpec(memory_space=pltpu.VMEM)
    hbm = pl.BlockSpec(memory_space=pltpu.HBM)
    rows = max(gs // 2 * rr, 256)
    rhs2 = rhs2.T
    scratch = [
        pltpu.VMEM((rr, held), F32),
        pltpu.VMEM((1, held), I32),
        pltpu.VMEM((1, held), I32),
        pltpu.VMEM((ni, ni), BF),
        pltpu.VMEM((ni, ns1), BF),
        pltpu.VMEM((ni, ns2), BF),
        pltpu.VMEM((2, nz) + f.shape, BF),
        pltpu.VMEM((2, nz) + v1.shape, BF),
        pltpu.VMEM(v2.shape, BF),
        pltpu.VMEM(rhs1.shape, F32),
        pltpu.VMEM(rhs2.shape, F32),
        pltpu.VMEM((256, 128), BF),
        pltpu.VMEM((CHUNK, CHUNK + 128), BF),
        pltpu.VMEM((2 * SLOTS, held), BF),
        pltpu.VMEM((16, held), BF),
        pltpu.VMEM((rr, held), BF),
        pltpu.VMEM((rows, WIDE), BF),
        pltpu.VMEM((256, LAND), BF),
        pltpu.VMEM((rows, 256), F32),
        pltpu.VMEM((nd, 256), F32),
        pltpu.VMEM((nd, 128), F32),
        pltpu.VMEM((nx, gs, rr, SLOTS), BF),
        pltpu.VMEM((nd, 1, SLOTS), F32),
        pltpu.VMEM((nx, gs, rr, SLOTS), BF),
        pltpu.VMEM((nx, gs, 1, SLOTS), F32),
        pltpu.VMEM((rr, ni), F32),
        pltpu.VMEM((2, nx, ny, nz, 2 * v2.shape[0], ns2 // 2), BF),
        pltpu.VMEM((ns2, ns2), BF),
        pltpu.VMEM((128, 128), F32),
        pltpu.VMEM((rr, ns1), F32),
        pltpu.VMEM((rr, ns2), F32),
        pltpu.VMEM((nby, rr, ns1), BF),
        pltpu.VMEM((nby, rr, 128), BF),
        pltpu.VMEM((nby, rr, 128), BF),
        pltpu.VMEM((nbx, rr, 128), BF),
        pltpu.VMEM((nby, rr, 128), BF),
        pltpu.SemaphoreType.DMA((11,)),
        pltpu.SemaphoreType.DMA((nx,)),
        pltpu.SemaphoreType.DMA((nx,)),
        pltpu.SemaphoreType.DMA((nx,)),
        pltpu.SemaphoreType.DMA((nx,)),
        pltpu.SemaphoreType.DMA((12,)),
        pltpu.SemaphoreType.DMA((12,)),
    ]
    shapes = (
        jax.ShapeDtypeStruct((rr, ni), F32),
        jax.ShapeDtypeStruct((rr, ns1), F32),
        jax.ShapeDtypeStruct((rr, ns2), F32),
    )
    outs = pl.pallas_call(
        functools.partial(kernel, nbx, nby),
        out_shape=shapes,
        in_specs=[hbm] * 11,
        out_specs=(vmem,) * 3,
        scratch_shapes=scratch,
        compiler_params=pltpu.CompilerParams(
            collective_id=0, has_side_effects=True, vmem_limit_bytes=46 << 20
        ),
    )(*[
        pltpu.with_memory_space_constraint(v, pltpu.HBM) for v in (
            sens, owner.reshape(1, held), cell.reshape(1, held), g.reshape(ni, ni),
            c, e, f, v1, v2, rhs1, rhs2,
        )
    ])
    return pl.pallas_call(
        store,
        out_shape=shapes,
        in_specs=[vmem] * 3,
        out_specs=(hbm,) * 3,
        scratch_shapes=[pltpu.SemaphoreType.DMA((3,))],
        compiler_params=pltpu.CompilerParams(vmem_limit_bytes=2 << 20),
    )(*outs)


def solution(mesh):
    nbx, nby = mesh.shape["bx"], mesh.shape["by"]
    both = ("bx", "by")
    in_specs = (
        P(None, both), P(both, None), P(both), P(both, None, None),
        P(both, None), P(both, None), P(both, None), P(both, None), P(both, None),
        P(None, both), P(None, both),
    )
    out_specs = (P(None, both), P(None, "bx"), P())
    return jax.shard_map(
        functools.partial(body, nbx, nby), mesh=mesh, in_specs=in_specs, out_specs=out_specs,
        check_vma=False,
    )
```

```python
import functools

import jax
import jax.numpy as jnp
from jax import lax
from jax.experimental import pallas as pl
from jax.experimental.pallas import tpu as pltpu
from jax.sharding import PartitionSpec as P

BF = jnp.bfloat16
F32 = jnp.float32
I32 = jnp.int32
MESH = pl.DeviceIdType.MESH
SLOTS = 128
CHUNK = 256
WIDE = 2048
LAND = 2048


def nn(a, b):
    return jnp.dot(a, b, preferred_element_type=F32)


def nt(a, b):
    return lax.dot_general(a, b, (((1,), (1,)), ((), ())), preferred_element_type=F32)


def hot(mask):
    return jnp.where(mask, jnp.ones((), BF), jnp.zeros((), BF))


def rows16(row, count=16):
    return jnp.broadcast_to(row.astype(F32), (count, row.shape[1])).astype(BF)


def chip_groups(nx, ny, nz):
    def key(offset):
        hops = [min(d, n - d) for d, n in zip(offset, (nx, ny, nz))]
        sign = sum(d == 3 for d in offset)
        if sorted(hops) == [0, 1, 2]:
            sign += (hops.index(1) - hops.index(2)) % 3 == 1
        late = sign % 2 == 0 and sorted(hops) != [0, 2, 2]
        return -sum(hops), late

    offsets = sorted(
        ((i, j, k) for i in range(nx) for j in range(ny) for k in range(nz)), key=key
    )
    size = len(offsets) // nx
    return [offsets[t * size : (t + 1) * size] for t in range(nx)]


def kernel(
    nbx, nby,
    sens_h, owner_h, cell_h, g_h, c_h, e_h, f_h, v1_h, v2_h, rhs1_h, rhs2_h,
    filt, s1o, s2o,
    sens, owner, cell, g, c, e, ff, vv, v2s, rhs1, rhs2,
    io, up, lt, hb, vb, a, cl, acc, acc3, base, packed, pcell, recv, rcell,
    ly, v2x, v2f, pad, p1, p2, ex1, ex3s, ex3, ex4, ex5,
    load_sem, send_v, send_c, recv_v, recv_c, ssem, rsem,
):
    nx = 4 if nbx == 16 else 2
    ny = nbx // nx
    nz = nby // 2
    nd = nbx * nby
    gs = nd // nx
    hg = gs // 2
    nh = nd // 2
    rr, held = sens.shape
    bx = lax.axis_index("bx")
    by = lax.axis_index("by")
    me = bx * nby + by
    x, y = bx // ny, lax.rem(bx, ny)
    z, core = by // 2, lax.rem(by, 2)
    outer = x * (1 - core) + y * core
    inner = y * (1 - core) + x * core

    def bx_of(far, near):
        return far * (ny * (1 - core) + core) + near * ((1 - core) + ny * core)

    loads = []
    pairs = (
        (owner_h, owner), (cell_h, cell), (sens_h, sens), (v2_h, v2s),
        (f_h, ff.at[core, z]), (v1_h, vv.at[core, z]), (rhs1_h, rhs1), (rhs2_h, rhs2),
        (c_h, c), (e_h, e), (g_h, g),
    )
    for k, (src, dst) in enumerate(pairs):
        cp = pltpu.make_async_copy(src, dst, load_sem.at[k])
        cp.start()
        loads.append(cp)

    barrier = pltpu.get_barrier_semaphore()

    bys = [lax.rem(by + j, nby) for j in range(nby)]

    def greet(bxt, targets):
        for byt in targets:
            pl.semaphore_signal(barrier, inc=1, device_id=(bxt, byt), device_id_type=MESH)

    def greet_step(i, _):
        greet(lax.rem(bx + i, nbx), bys)
        return 0

    greet(bx, bys[1:])
    lax.fori_loop(1, nbx, greet_step, 0)

    io[...] = lax.broadcasted_iota(I32, (256, 128), 0).astype(F32).astype(BF)
    up[:, 0:CHUNK] = jnp.where(
        lax.broadcasted_iota(I32, (CHUNK, CHUNK), 0)
        < lax.broadcasted_iota(I32, (CHUNK, CHUNK), 1),
        1.0, 0.0,
    ).astype(BF)
    up[:, CHUNK:] = jnp.ones((CHUNK, 128), BF)

    def counting(first, count, lanes):
        block = io[first : first + count, :]
        return jnp.concatenate([block] * (lanes // 128), axis=1)

    base[...] = jnp.zeros_like(base)
    acc3[...] = jnp.zeros_like(acc3)
    for cp in loads[0:3]:
        cp.wait()
    nb = min(16, nh)

    def rank_chunk(ks):
        own = owner[:, ks]
        ob = rows16(own)
        dtb = jnp.concatenate(
            [hot(counting(i, min(16, nd), CHUNK) == ob[0 : min(16, nd)]) for i in range(0, nd, 16)],
            axis=0,
        )
        pre = nn(dtb, up[...])
        b = base[...]
        m = lax.broadcasted_iota(I32, (nd, CHUNK), 0) == own
        ranked = pre[:, 0:CHUNK] + jnp.concatenate([b, b], axis=1)
        pos = jnp.sum(jnp.where(m, ranked, 0.0), axis=0, keepdims=True)
        base[...] = b + pre[:, CHUNK:]
        sb = rows16(pos + (SLOTS * (own & 1)).astype(F32))
        for i in range(0, 2 * SLOTS, 16):
            lt[i : i + 16, ks] = hot(counting(i, 16, CHUNK) == sb)
        hk = rows16(own >> 1)
        hb[:, ks] = hk
        vb[:, ks] = sens[:, ks].astype(BF)
        ce = cell[:, ks]
        hi = rows16(ce >> 8)
        lo = rows16(ce & 255)
        ms = [counting(i, nb, CHUNK) == hk[0:nb] for i in range(0, nh, nb)]
        a3 = [jnp.where(m3, w[0:nb], jnp.zeros((), BF)) for w in (hi, lo) for m3 in ms]
        return jnp.concatenate(a3, axis=0)

    def rank_step(k, _):
        a3 = []
        for q in range(4):
            a3.append(rank_chunk(pl.ds(pl.multiple_of((k * 4 + q) * CHUNK, CHUNK), CHUNK)))
        ks = pl.ds(pl.multiple_of(k * 4 * CHUNK, 4 * CHUNK), 4 * CHUNK)
        acc3[...] += nt(jnp.concatenate(a3, axis=1), lt[:, ks])
        return 0

    rank_steps = held // (4 * CHUNK)
    early = rank_steps * 3 // 4
    lax.fori_loop(0, early, rank_step, 0)

    for cp in loads[3:6]:
        cp.wait()
    r2 = v2s.shape[0]
    half2 = v2s.shape[1] // 2
    v2v = v2s[...].astype(F32)
    v2x[core, outer, inner, z] = jnp.concatenate(
        [v2v[:, 0:half2], v2v[:, half2:]], axis=0
    ).astype(BF)

    def remote(src, dst, k, where):
        pltpu.make_async_remote_copy(
            src, dst, ssem.at[k], rsem.at[k], device_id=where, device_id_type=MESH
        ).start()

    def came(k, ref):
        pltpu.make_async_copy(ref, ref, rsem.at[k]).wait()

    def went(k, ref):
        pltpu.make_async_copy(ref, ref, ssem.at[k]).wait()

    pl.semaphore_wait(barrier, nd - 1)

    frows = ff.shape[2] // 2
    own_top = v2x.at[core, outer, inner]
    own_sep = vv.at[core]
    stage_z = (
        (0, own_top.at[z], own_top.at[pl.ds(0, max(nz - 1, 1))]),
        (1, ff.at[core, z, pl.ds(0, frows)], ff.at[core, pl.ds(0, max(nz - 1, 1)), pl.ds(0, frows)]),
        (2, own_sep.at[z], own_sep.at[pl.ds(0, max(nz - 1, 1))]),
        (12, ff.at[core, z, pl.ds(frows, frows)], ff.at[core, pl.ds(0, max(nz - 1, 1)), pl.ds(0, frows)]),
    )

    def gather_z(*which):
        for n in which:
            k, part, _ = stage_z[n]
            for r in range(1, nz):
                remote(part, part, k, (bx, lax.rem(z + r, nz) * 2 + core))

    def gather_inner():
        if nz > 1:
            came(0, stage_z[0][2])
        blk = v2x.at[core, outer, inner]
        for r in range(1, ny):
            remote(blk, blk, 3, (bx_of(outer, lax.rem(inner + r, ny)), by))

    def gather_outer():
        came(3, v2x.at[core, outer, pl.ds(0, ny - 1)])
        blk = v2x.at[core, outer]
        for r in range(1, nx):
            remote(blk, blk, 4, (bx_of(lax.rem(outer + r, nx), inner), by))

    partner = (bx, z * 2 + 1 - core)

    def gather_pair():
        if nz > 1:
            for k, _, rest_of in stage_z[1:]:
                came(k, rest_of)
        for k, buf in ((5, ff), (6, vv)):
            remote(buf.at[core], buf.at[core], k, partner)

    def gather_top():
        came(4, v2x.at[core, pl.ds(0, nx - 1)])
        remote(v2x.at[core], v2x.at[core], 7, partner)

    gather_z(0, 1, 2)
    lax.fori_loop(early, rank_steps, rank_step, 0)
    cells = acc3[0:nh, :] * 256.0 + acc3[nh : 2 * nh, :]
    for h in range(nh):
        for half in range(2):
            pcell[2 * h + half] = cells[h : h + 1, half * SLOTS : (half + 1) * SLOTS]

    groups = chip_groups(nx, ny, nz)
    last = nx - 1
    xs = [lax.rem(x + k, nx) for k in range(nx)]
    ys = [lax.rem(y + k, ny) for k in range(ny)]
    zs = [lax.rem(z + k, nz) for k in range(nz)]
    steps = max(held // WIDE, 1)
    wide = held // steps

    def chip_at(offset):
        return (xs[offset[0]] * ny + ys[offset[1]]) * nz + zs[offset[2]]

    def send(gi, k, core_to):
        offset = groups[gi][k]
        to = (xs[offset[0]] * ny + ys[offset[1]], zs[offset[2]] * 2 + core_to)
        pltpu.make_async_remote_copy(
            packed.at[gi, 2 * k + core_to], recv.at[gi, 2 * k + core],
            send_v.at[gi], recv_v.at[gi], device_id=to, device_id_type=MESH,
        ).start()
        pltpu.make_async_remote_copy(
            pcell.at[chip_at(offset) * 2 + core_to], rcell.at[gi, 2 * k + core],
            send_c.at[gi], recv_c.at[gi], device_id=to, device_id_type=MESH,
        ).start()

    def send_group(gi):
        for k in range(hg):
            if gi == last and k == hg - 1:
                send(gi, k, 1 - core)
            else:
                send(gi, k, 0)
                send(gi, k, 1)

    def pack(gi):
        chips = [chip_at(offset).astype(F32).astype(BF) for offset in groups[gi]]
        acc[...] = jnp.zeros_like(acc)

        def pack_step(k, _, sends=False):
            ks = pl.ds(pl.multiple_of(k * wide, wide), wide)
            if sends:
                send_group(gi - 1)
            hk = hb[:, ks]
            for h in range(hg):
                m = hk == chips[h]
                for q in range(rr // 16):
                    rows = slice(h * rr + q * 16, h * rr + q * 16 + 16)
                    a[rows, 0:wide] = jnp.where(
                        m, vb[q * 16 : q * 16 + 16, ks], jnp.zeros((), BF)
                    )
            acc[0 : hg * rr, :] += nt(a[0 : hg * rr, 0:wide], lt[:, ks])
            return 0

        pack_step(0, 0, gi > 0)
        lax.fori_loop(1, steps, pack_step, 0)
        for h in range(hg):
            for half in range(2):
                packed[gi, 2 * h + half] = acc[
                    h * rr : (h + 1) * rr, half * SLOTS : (half + 1) * SLOTS
                ].astype(BF)

    for gi in range(nx):
        pack(gi)
    send_group(last)
    gather_z(3)
    gather_inner()
    recv[last, gs - 2 + core] = packed[last, gs - 2 + core]
    rcell[last, gs - 2 + core] = pcell[me]

    ncell = 2048 // 256
    pieces = min(LAND // SLOTS, gs)
    acc[0:256, :] = jnp.zeros((256, 256), F32)

    def land(gi):
        n = gs - 1 if gi == last else gs
        got = recv.at[gi, pl.ds(0, n)]
        pltpu.make_async_copy(got, got, recv_v.at[gi]).wait()
        got = rcell.at[gi, pl.ds(0, n)]
        pltpu.make_async_copy(got, got, recv_c.at[gi]).wait()

        def land_step(s, _):
            for p in range(pieces):
                ci = rcell[gi, s * pieces + p].astype(I32)
                lanes = slice(p * SLOTS, (p + 1) * SLOTS)
                lob = rows16(ci & 255)
                hib = rows16(ci >> 8)
                for i in range(0, 256, 16):
                    cl[i : i + 16, lanes] = hot(io[i : i + 16, :] == lob)
                blk = recv[gi, s * pieces + p]
                for ch in range(ncell):
                    m = hib == jnp.asarray(ch, BF)
                    for q in range(rr // 16):
                        rows = slice(ch * rr + q * 16, ch * rr + q * 16 + 16)
                        a[rows, lanes] = jnp.where(
                            m, blk[q * 16 : q * 16 + 16, :], jnp.zeros((), BF)
                        )
            wide_k = slice(0, pieces * SLOTS)
            acc[0:256, :] += nt(a[0:256, wide_k], cl[:, wide_k])
            return 0

        lax.fori_loop(0, gs // pieces, land_step, 0)

    for gi in range(nx):
        land(gi)
    gather_outer()

    gather_pair()
    load = jnp.concatenate(
        [acc[ch * rr : (ch + 1) * rr, :].astype(BF) for ch in range(ncell)], axis=1
    )

    for cp in loads[6:]:
        cp.wait()
    ni = g.shape[0]
    tiles = [slice(n, n + 512) for n in range(0, ni, 512)]
    for cols in tiles:
        ly[:, cols] = nn(load, g[:, cols])
    lyb = ly[...].astype(BF)

    def placed(part, rhs, share, index):
        per_block = 128 // share
        turned = pltpu.roll(rhs, lax.rem(index, per_block) * share, 1)
        at = pl.ds(pl.multiple_of((index // per_block) * 128, 128), 128)
        part[:, at] = part[:, at] + turned

    def spread(k, src_of, dst):
        for r in range(1, nby):
            j = lax.rem(by + r, nby)
            remote(src_of(j), dst, k, (bx, j))

    def total(buf):
        out = buf[0].astype(F32)
        for j in range(1, buf.shape[0]):
            out = out + buf[j].astype(F32)
        return out

    p1[...] = -nn(lyb, c[...])
    pad[...] = jnp.zeros_like(pad)
    pad[0:rr, 0 : rhs1.shape[1]] = rhs1[...]
    placed(p1, pad[0:rr, :], rhs1.shape[1], by)
    ex1[by] = p1[...].astype(BF)
    u = ex1[by]
    p2[...] = -nn(lyb, e[...])
    pad[...] = jnp.zeros_like(pad)
    pad[0 : rhs2.shape[0], 0:rr] = rhs2[...]
    placed(p2, pad[...].T[0:rr, :], rhs2.shape[0], me)

    came(5, ff.at[core])
    came(6, vv.at[core])
    ns1, ns2 = p1.shape[1], p2.shape[1]
    v1 = vv[...].reshape(ns1, ns1)
    f = ff[...].reshape(ns1, ns2)
    part2 = p2[...] - nn(nt(u, v1).astype(BF), f)
    for j in range(nby):
        ex3s[j] = part2[:, j * 128 : (j + 1) * 128].astype(BF)
    spread(9, lambda j: ex3s.at[j], ex3.at[by])
    spread(8, lambda j: ex1.at[by], ex1.at[by])
    ex3[by] = ex3s[by]

    came(9, ex3.at[pl.ds(0, nby - 1)])
    ex4[bx] = total(ex3).astype(BF)
    for r in range(1, nbx):
        remote(ex4.at[bx], ex4.at[bx], 10, (lax.rem(bx + r, nbx), by))
    gather_top()
    came(8, ex1.at[pl.ds(0, nby - 1)])
    s1y = nt(total(ex1).astype(BF), v1)
    came(10, ex4.at[pl.ds(0, nbx - 1)])
    ex5[by] = total(ex4).astype(BF)
    spread(11, lambda j: ex5.at[by], ex5.at[by])
    came(7, v2x.at[core])
    some = ny * nz

    def turn_step(k, _):
        blocks = v2x[k // nx, lax.rem(k, nx)].astype(F32).reshape(some, 2 * r2, half2)
        at = pl.ds(pl.multiple_of(k * some * r2, some * r2), some * r2)
        v2f[at, 0:half2] = blocks[:, 0:r2].reshape(some * r2, half2).astype(BF)
        v2f[at, half2:] = blocks[:, r2:].reshape(some * r2, half2).astype(BF)
        return 0

    lax.fori_loop(0, 2 * nx, turn_step, 0)

    came(11, ex5.at[pl.ds(0, nby - 1)])
    z2b = jnp.concatenate([ex5[j] for j in range(nby)], axis=1)

    y2 = nt(z2b, v2f[...]).astype(BF)
    s2 = nn(y2, v2f[...])
    s2o[...] = s2
    s2b = s2.astype(BF)
    back1 = s1y - nt(s2b, f)
    s1 = nn(back1.astype(BF), v1)
    s1o[...] = s1
    s1b = s1.astype(BF)
    for cols in tiles:
        ly[:, cols] = ly[:, cols] - nt(s1b, c[cols, :]) - nt(s2b, e[cols, :])
    rest = ly[...].astype(BF)
    for cols in tiles:
        filt[:, cols] = nt(rest, g[cols, :])

    if nz > 1:
        for k, _, rest_of in stage_z:
            went(k, rest_of)
    went(3, v2x.at[core, outer, pl.ds(0, ny - 1)])
    went(4, v2x.at[core, pl.ds(0, nx - 1)])
    for k, buf in ((5, ff), (6, vv), (7, v2x)):
        went(k, buf.at[core])
    went(8, ex1.at[pl.ds(0, nby - 1)])
    went(9, ex3.at[pl.ds(0, nby - 1)])
    went(10, ex4.at[pl.ds(0, nbx - 1)])
    went(11, ex5.at[pl.ds(0, nby - 1)])
    for gi in range(nx):
        n = gs - 1 if gi == last else gs
        got = packed.at[gi, pl.ds(0, n)]
        pltpu.make_async_copy(got, got, send_v.at[gi]).wait()
        got = rcell.at[gi, pl.ds(0, n)]
        pltpu.make_async_copy(got, got, send_c.at[gi]).wait()


def store(filt, s1, s2, filt_h, s1_h, s2_h, sem):
    copies = [
        pltpu.make_async_copy(src, dst, sem.at[k])
        for k, (src, dst) in enumerate(((filt, filt_h), (s1, s1_h), (s2, s2_h)))
    ]
    for cp in copies:
        cp.start()
    for cp in copies:
        cp.wait()


def body(nbx, nby, sens, owner, cell, g, c, e, f, v1, v2, rhs1, rhs2):
    nx = 4 if nbx == 16 else 2
    ny, nz = nbx // nx, nby // 2
    nd = nbx * nby
    gs = nd // nx
    rr, held = sens.shape
    ni = g.shape[1]
    ns1 = c.shape[1]
    ns2 = e.shape[1]
    vmem = pl.BlockSpec(memory_space=pltpu.VMEM)
    hbm = pl.BlockSpec(memory_space=pltpu.HBM)
    rows = max(gs // 2 * rr, 256)
    rhs2 = rhs2.T
    scratch = [
        pltpu.VMEM((rr, held), F32),
        pltpu.VMEM((1, held), I32),
        pltpu.VMEM((1, held), I32),
        pltpu.VMEM((ni, ni), BF),
        pltpu.VMEM((ni, ns1), BF),
        pltpu.VMEM((ni, ns2), BF),
        pltpu.VMEM((2, nz) + f.shape, BF),
        pltpu.VMEM((2, nz) + v1.shape, BF),
        pltpu.VMEM(v2.shape, BF),
        pltpu.VMEM(rhs1.shape, F32),
        pltpu.VMEM(rhs2.shape, F32),
        pltpu.VMEM((256, 128), BF),
        pltpu.VMEM((CHUNK, CHUNK + 128), BF),
        pltpu.VMEM((2 * SLOTS, held), BF),
        pltpu.VMEM((16, held), BF),
        pltpu.VMEM((rr, held), BF),
        pltpu.VMEM((rows, WIDE), BF),
        pltpu.VMEM((256, LAND), BF),
        pltpu.VMEM((rows, 256), F32),
        pltpu.VMEM((nd, 256), F32),
        pltpu.VMEM((nd, 128), F32),
        pltpu.VMEM((nx, gs, rr, SLOTS), BF),
        pltpu.VMEM((nd, 1, SLOTS), F32),
        pltpu.VMEM((nx, gs, rr, SLOTS), BF),
        pltpu.VMEM((nx, gs, 1, SLOTS), F32),
        pltpu.VMEM((rr, ni), F32),
        pltpu.VMEM((2, nx, ny, nz, 2 * v2.shape[0], ns2 // 2), BF),
        pltpu.VMEM((ns2, ns2), BF),
        pltpu.VMEM((128, 128), F32),
        pltpu.VMEM((rr, ns1), F32),
        pltpu.VMEM((rr, ns2), F32),
        pltpu.VMEM((nby, rr, ns1), BF),
        pltpu.VMEM((nby, rr, 128), BF),
        pltpu.VMEM((nby, rr, 128), BF),
        pltpu.VMEM((nbx, rr, 128), BF),
        pltpu.VMEM((nby, rr, 128), BF),
        pltpu.SemaphoreType.DMA((11,)),
        pltpu.SemaphoreType.DMA((nx,)),
        pltpu.SemaphoreType.DMA((nx,)),
        pltpu.SemaphoreType.DMA((nx,)),
        pltpu.SemaphoreType.DMA((nx,)),
        pltpu.SemaphoreType.DMA((13,)),
        pltpu.SemaphoreType.DMA((13,)),
    ]
    shapes = (
        jax.ShapeDtypeStruct((rr, ni), F32),
        jax.ShapeDtypeStruct((rr, ns1), F32),
        jax.ShapeDtypeStruct((rr, ns2), F32),
    )
    outs = pl.pallas_call(
        functools.partial(kernel, nbx, nby),
        out_shape=shapes,
        in_specs=[hbm] * 11,
        out_specs=(vmem,) * 3,
        scratch_shapes=scratch,
        compiler_params=pltpu.CompilerParams(
            collective_id=0, has_side_effects=True, vmem_limit_bytes=46 << 20
        ),
    )(*[
        pltpu.with_memory_space_constraint(v, pltpu.HBM) for v in (
            sens, owner.reshape(1, held), cell.reshape(1, held), g.reshape(ni, ni),
            c, e, f, v1, v2, rhs1, rhs2,
        )
    ])
    return pl.pallas_call(
        store,
        out_shape=shapes,
        in_specs=[vmem] * 3,
        out_specs=(hbm,) * 3,
        scratch_shapes=[pltpu.SemaphoreType.DMA((3,))],
        compiler_params=pltpu.CompilerParams(vmem_limit_bytes=2 << 20),
    )(*outs)


def solution(mesh):
    nbx, nby = mesh.shape["bx"], mesh.shape["by"]
    both = ("bx", "by")
    in_specs = (
        P(None, both), P(both, None), P(both), P(both, None, None),
        P(both, None), P(both, None), P(both, None), P(both, None), P(both, None),
        P(None, both), P(None, both),
    )
    out_specs = (P(None, both), P(None, "bx"), P())
    return jax.shard_map(
        functools.partial(body, nbx, nby), mesh=mesh, in_specs=in_specs, out_specs=out_specs,
        check_vma=False,
    )
```

```python
import functools

import jax
import jax.numpy as jnp
from jax import lax
from jax.experimental import pallas as pl
from jax.experimental.pallas import tpu as pltpu
from jax.sharding import PartitionSpec as P

BF = jnp.bfloat16
F32 = jnp.float32
I32 = jnp.int32
MESH = pl.DeviceIdType.MESH
SLOTS = 128
CHUNK = 256
WIDE = 2048
LAND = 2048


def nn(a, b):
    return jnp.dot(a, b, preferred_element_type=F32)


def nt(a, b):
    return lax.dot_general(a, b, (((1,), (1,)), ((), ())), preferred_element_type=F32)


def hot(mask):
    return jnp.where(mask, jnp.ones((), BF), jnp.zeros((), BF))


def rows16(row, count=16):
    return jnp.broadcast_to(row.astype(F32), (count, row.shape[1])).astype(BF)


def columns(row):
    return rows16(row, 128).T


def chip_groups(nx, ny, nz):
    def key(offset):
        hops = [min(d, n - d) for d, n in zip(offset, (nx, ny, nz))]
        sign = sum(d == 3 for d in offset)
        if sorted(hops) == [0, 1, 2]:
            sign += (hops.index(1) - hops.index(2)) % 3 == 1
        late = sign % 2 == 0 and sorted(hops) != [0, 2, 2]
        return -sum(hops), late

    offsets = sorted(
        ((i, j, k) for i in range(nx) for j in range(ny) for k in range(nz)), key=key
    )
    size = len(offsets) // nx
    return [offsets[t * size : (t + 1) * size] for t in range(nx)]


def kernel(
    nbx, nby,
    sens_h, owner_h, cell_h, g_h, c_h, e_h, f_h, v1_h, v2_h, rhs1_h, rhs2_h,
    filt, s1o, s2o,
    sens, owner, cell, g, c, e, ff, vv, v2s, rhs1, rhs2,
    io, il, up, lt, hb, vb, a, cl, acc, acc3, base, packed, pcell, recv, rcell,
    gt, ct, et, ly, v2x, v2f, pad, p1, p2, ex1, ex3s, ex3, ex4, ex5,
    load_sem, send_v, send_c, recv_v, recv_c, ssem, rsem,
):
    nx = 4 if nbx == 16 else 2
    ny = nbx // nx
    nz = nby // 2
    nd = nbx * nby
    gs = nd // nx
    hg = gs // 2
    nh = nd // 2
    rr, held = sens.shape
    bx = lax.axis_index("bx")
    by = lax.axis_index("by")
    me = bx * nby + by
    x, y = bx // ny, lax.rem(bx, ny)
    z, core = by // 2, lax.rem(by, 2)
    outer = x * (1 - core) + y * core
    inner = y * (1 - core) + x * core

    def bx_of(far, near):
        return far * (ny * (1 - core) + core) + near * ((1 - core) + ny * core)

    loads = []
    pairs = (
        (owner_h, owner), (cell_h, cell), (sens_h, sens), (v2_h, v2s),
        (f_h, ff.at[core, z]), (v1_h, vv.at[core, z]), (rhs1_h, rhs1), (rhs2_h, rhs2),
        (c_h, c), (e_h, e), (g_h, g),
    )
    for k, (src, dst) in enumerate(pairs):
        cp = pltpu.make_async_copy(src, dst, load_sem.at[k])
        cp.start()
        loads.append(cp)

    barrier = pltpu.get_barrier_semaphore()

    bys = [lax.rem(by + j, nby) for j in range(nby)]

    def greet(bxt, targets):
        for byt in targets:
            pl.semaphore_signal(barrier, inc=1, device_id=(bxt, byt), device_id_type=MESH)

    def greet_step(i, _):
        greet(lax.rem(bx + i, nbx), bys)
        return 0

    greet(bx, bys[1:])
    lax.fori_loop(1, nbx, greet_step, 0)

    io[...] = lax.broadcasted_iota(I32, (256, 128), 0).astype(F32).astype(BF)
    il[...] = lax.broadcasted_iota(I32, (CHUNK, 2 * SLOTS), 1).astype(F32).astype(BF)
    up[:, 0:CHUNK] = jnp.where(
        lax.broadcasted_iota(I32, (CHUNK, CHUNK), 0)
        < lax.broadcasted_iota(I32, (CHUNK, CHUNK), 1),
        1.0, 0.0,
    ).astype(BF)
    up[:, CHUNK:] = jnp.ones((CHUNK, 128), BF)

    def counting(first, count, lanes):
        block = io[first : first + count, :]
        return jnp.concatenate([block] * (lanes // 128), axis=1)

    base[...] = jnp.zeros_like(base)
    acc3[...] = jnp.zeros_like(acc3)
    for cp in loads[0:3]:
        cp.wait()
    nb = min(16, nh)

    def rank_chunk(ks):
        own = owner[:, ks]
        ob = rows16(own)
        dtb = jnp.concatenate(
            [hot(counting(i, min(16, nd), CHUNK) == ob[0 : min(16, nd)]) for i in range(0, nd, 16)],
            axis=0,
        )
        pre = nn(dtb, up[...])
        b = base[...]
        m = lax.broadcasted_iota(I32, (nd, CHUNK), 0) == own
        ranked = pre[:, 0:CHUNK] + jnp.concatenate([b, b], axis=1)
        pos = jnp.sum(jnp.where(m, ranked, 0.0), axis=0, keepdims=True)
        base[...] = b + pre[:, CHUNK:]
        down = columns(pos + (SLOTS * (own & 1)).astype(F32))
        for half in range(2):
            lanes = slice(half * SLOTS, (half + 1) * SLOTS)
            lt[ks, lanes] = hot(il[:, lanes] == down)
        hk = rows16(own >> 1)
        hb[:, ks] = hk
        vb[:, ks] = sens[:, ks].astype(BF)
        ce = cell[:, ks]
        hi = rows16(ce >> 8)
        lo = rows16(ce & 255)
        ms = [counting(i, nb, CHUNK) == hk[0:nb] for i in range(0, nh, nb)]
        a3 = [jnp.where(m3, w[0:nb], jnp.zeros((), BF)) for w in (hi, lo) for m3 in ms]
        return jnp.concatenate(a3, axis=0)

    def rank_step(k, _):
        a3 = []
        for q in range(4):
            a3.append(rank_chunk(pl.ds(pl.multiple_of((k * 4 + q) * CHUNK, CHUNK), CHUNK)))
        ks = pl.ds(pl.multiple_of(k * 4 * CHUNK, 4 * CHUNK), 4 * CHUNK)
        acc3[...] += nn(jnp.concatenate(a3, axis=1), lt[ks, :])
        return 0

    rank_steps = held // (4 * CHUNK)
    early = rank_steps * 3 // 4
    lax.fori_loop(0, early, rank_step, 0)

    for cp in loads[3:6]:
        cp.wait()
    r2 = v2s.shape[0]
    half2 = v2s.shape[1] // 2
    v2v = v2s[...].astype(F32)
    v2x[core, outer, inner, z] = jnp.concatenate(
        [v2v[:, 0:half2], v2v[:, half2:]], axis=0
    ).astype(BF)

    def remote(src, dst, k, where):
        pltpu.make_async_remote_copy(
            src, dst, ssem.at[k], rsem.at[k], device_id=where, device_id_type=MESH
        ).start()

    def came(k, ref):
        pltpu.make_async_copy(ref, ref, rsem.at[k]).wait()

    def went(k, ref):
        pltpu.make_async_copy(ref, ref, ssem.at[k]).wait()

    pl.semaphore_wait(barrier, nd - 1)

    frows = ff.shape[2] // 2
    own_top = v2x.at[core, outer, inner]
    own_sep = vv.at[core]
    stage_z = (
        (0, own_top.at[z], own_top.at[pl.ds(0, max(nz - 1, 1))]),
        (1, ff.at[core, z, pl.ds(0, frows)], ff.at[core, pl.ds(0, max(nz - 1, 1)), pl.ds(0, frows)]),
        (2, own_sep.at[z], own_sep.at[pl.ds(0, max(nz - 1, 1))]),
        (12, ff.at[core, z, pl.ds(frows, frows)], ff.at[core, pl.ds(0, max(nz - 1, 1)), pl.ds(0, frows)]),
    )

    def gather_z(*which):
        for n in which:
            k, part, _ = stage_z[n]
            for r in range(1, nz):
                remote(part, part, k, (bx, lax.rem(z + r, nz) * 2 + core))

    def gather_inner():
        if nz > 1:
            came(0, stage_z[0][2])
        blk = v2x.at[core, outer, inner]
        for r in range(1, ny):
            remote(blk, blk, 3, (bx_of(outer, lax.rem(inner + r, ny)), by))

    def gather_outer():
        came(3, v2x.at[core, outer, pl.ds(0, ny - 1)])
        blk = v2x.at[core, outer]
        for r in range(1, nx):
            remote(blk, blk, 4, (bx_of(lax.rem(outer + r, nx), inner), by))

    partner = (bx, z * 2 + 1 - core)

    def gather_pair():
        if nz > 1:
            for k, _, rest_of in stage_z[1:]:
                came(k, rest_of)
        for k, buf in ((5, ff), (6, vv)):
            remote(buf.at[core], buf.at[core], k, partner)

    def gather_top():
        came(4, v2x.at[core, pl.ds(0, nx - 1)])
        remote(v2x.at[core], v2x.at[core], 7, partner)

    gather_z(0, 1, 2)
    lax.fori_loop(early, rank_steps, rank_step, 0)
    cells = acc3[0:nh, :] * 256.0 + acc3[nh : 2 * nh, :]
    for h in range(nh):
        for half in range(2):
            pcell[2 * h + half] = cells[h : h + 1, half * SLOTS : (half + 1) * SLOTS]

    groups = chip_groups(nx, ny, nz)
    last = nx - 1
    xs = [lax.rem(x + k, nx) for k in range(nx)]
    ys = [lax.rem(y + k, ny) for k in range(ny)]
    zs = [lax.rem(z + k, nz) for k in range(nz)]
    steps = max(held // WIDE, 1)
    wide = held // steps

    def chip_at(offset):
        return (xs[offset[0]] * ny + ys[offset[1]]) * nz + zs[offset[2]]

    def send(gi, k, core_to):
        offset = groups[gi][k]
        to = (xs[offset[0]] * ny + ys[offset[1]], zs[offset[2]] * 2 + core_to)
        pltpu.make_async_remote_copy(
            packed.at[gi, 2 * k + core_to], recv.at[gi, 2 * k + core],
            send_v.at[gi], recv_v.at[gi], device_id=to, device_id_type=MESH,
        ).start()
        pltpu.make_async_remote_copy(
            pcell.at[chip_at(offset) * 2 + core_to], rcell.at[gi, 2 * k + core],
            send_c.at[gi], recv_c.at[gi], device_id=to, device_id_type=MESH,
        ).start()

    def send_group(gi):
        for k in range(hg):
            if gi == last and k == hg - 1:
                send(gi, k, 1 - core)
            else:
                send(gi, k, 0)
                send(gi, k, 1)

    def pack(gi):
        chips = [chip_at(offset).astype(F32).astype(BF) for offset in groups[gi]]

        def pack_step(k, _, starts=False):
            ks = pl.ds(pl.multiple_of(k * wide, wide), wide)
            if starts and gi > 0:
                send_group(gi - 1)
            hk = hb[:, ks]
            for h in range(hg):
                m = hk == chips[h]
                for q in range(rr // 16):
                    rows = slice(h * rr + q * 16, h * rr + q * 16 + 16)
                    a[rows, 0:wide] = jnp.where(
                        m, vb[q * 16 : q * 16 + 16, ks], jnp.zeros((), BF)
                    )
            part = nn(a[0 : hg * rr, 0:wide], lt[ks, :])
            if starts:
                acc[0 : hg * rr, :] = part
            else:
                acc[0 : hg * rr, :] += part
            return 0

        pack_step(0, 0, True)
        lax.fori_loop(1, steps, pack_step, 0)
        for h in range(hg):
            for half in range(2):
                packed[gi, 2 * h + half] = acc[
                    h * rr : (h + 1) * rr, half * SLOTS : (half + 1) * SLOTS
                ].astype(BF)

    for gi in range(nx):
        pack(gi)
    send_group(last)
    gather_z(3)
    gather_inner()
    recv[last, gs - 2 + core] = packed[last, gs - 2 + core]
    rcell[last, gs - 2 + core] = pcell[me]

    ncell = 2048 // 256
    pieces = min(LAND // SLOTS, gs)
    acc[0:256, :] = jnp.zeros((256, 256), F32)

    def land(gi):
        n = gs - 1 if gi == last else gs
        got = recv.at[gi, pl.ds(0, n)]
        pltpu.make_async_copy(got, got, recv_v.at[gi]).wait()
        got = rcell.at[gi, pl.ds(0, n)]
        pltpu.make_async_copy(got, got, recv_c.at[gi]).wait()

        def land_step(s, _):
            for p in range(pieces):
                ci = rcell[gi, s * pieces + p].astype(I32)
                lanes = slice(p * SLOTS, (p + 1) * SLOTS)
                down = columns(ci & 255)
                hib = rows16(ci >> 8)
                for half in range(2):
                    across = slice(half * SLOTS, (half + 1) * SLOTS)
                    cl[lanes, across] = hot(il[0:SLOTS, across] == down)
                blk = recv[gi, s * pieces + p]
                for ch in range(ncell):
                    m = hib == jnp.asarray(ch, BF)
                    for q in range(rr // 16):
                        rows = slice(ch * rr + q * 16, ch * rr + q * 16 + 16)
                        a[rows, lanes] = jnp.where(
                            m, blk[q * 16 : q * 16 + 16, :], jnp.zeros((), BF)
                        )
            wide_k = slice(0, pieces * SLOTS)
            acc[0:256, :] += nn(a[0:256, wide_k], cl[wide_k, :])
            return 0

        lax.fori_loop(0, gs // pieces, land_step, 0)

    for gi in range(nx):
        land(gi)
    gather_outer()

    gather_pair()
    load = jnp.concatenate(
        [acc[ch * rr : (ch + 1) * rr, :].astype(BF) for ch in range(ncell)], axis=1
    )

    for cp in loads[6:]:
        cp.wait()
    ni = g.shape[0]
    tiles = [slice(n, n + 512) for n in range(0, ni, 512)]
    for cols in tiles:
        ly[:, cols] = nn(load, g[:, cols])
    lyb = ly[...].astype(BF)

    def placed(part, rhs, share, index):
        per_block = 128 // share
        turned = pltpu.roll(rhs, lax.rem(index, per_block) * share, 1)
        at = pl.ds(pl.multiple_of((index // per_block) * 128, 128), 128)
        part[:, at] = part[:, at] + turned

    def spread(k, src_of, dst):
        for r in range(1, nby):
            j = lax.rem(by + r, nby)
            remote(src_of(j), dst, k, (bx, j))

    def total(buf):
        out = buf[0].astype(F32)
        for j in range(1, buf.shape[0]):
            out = out + buf[j].astype(F32)
        return out

    p1[...] = -nn(lyb, c[...])
    pad[...] = jnp.zeros_like(pad)
    pad[0:rr, 0 : rhs1.shape[1]] = rhs1[...]
    placed(p1, pad[0:rr, :], rhs1.shape[1], by)
    ex1[by] = p1[...].astype(BF)
    u = ex1[by]
    p2[...] = -nn(lyb, e[...])
    pad[...] = jnp.zeros_like(pad)
    pad[0 : rhs2.shape[0], 0:rr] = rhs2[...]
    placed(p2, pad[...].T[0:rr, :], rhs2.shape[0], me)

    came(5, ff.at[core])
    came(6, vv.at[core])
    ns1, ns2 = p1.shape[1], p2.shape[1]
    v1 = vv[...].reshape(ns1, ns1)
    f = ff[...].reshape(ns1, ns2)
    part2 = p2[...] - nn(nt(u, v1).astype(BF), f)
    for j in range(nby):
        ex3s[j] = part2[:, j * 128 : (j + 1) * 128].astype(BF)
    spread(9, lambda j: ex3s.at[j], ex3.at[by])
    spread(8, lambda j: ex1.at[by], ex1.at[by])
    ex3[by] = ex3s[by]

    def turn_rows(src, dst):
        def step(k, _):
            at = pl.ds(pl.multiple_of(k * 256, 256), 256)
            for n in range(0, src.shape[1], 256):
                width = min(256, src.shape[1] - n)
                dst[n : n + width, at] = src[at, n : n + width].T
            return 0

        lax.fori_loop(0, src.shape[0] // 256, step, 0)

    turn_rows(c, ct)
    turn_rows(e, et)
    came(9, ex3.at[pl.ds(0, nby - 1)])
    ex4[bx] = total(ex3).astype(BF)
    for r in range(1, nbx):
        remote(ex4.at[bx], ex4.at[bx], 10, (lax.rem(bx + r, nbx), by))
    gather_top()
    came(8, ex1.at[pl.ds(0, nby - 1)])
    s1y = nt(total(ex1).astype(BF), v1)
    turn_rows(g, gt)
    came(10, ex4.at[pl.ds(0, nbx - 1)])
    ex5[by] = total(ex4).astype(BF)
    spread(11, lambda j: ex5.at[by], ex5.at[by])
    came(7, v2x.at[core])
    some = ny * nz

    def turn_step(k, _):
        blocks = v2x[k // nx, lax.rem(k, nx)].astype(F32).reshape(some, 2 * r2, half2)
        at = pl.ds(pl.multiple_of(k * some * r2, some * r2), some * r2)
        v2f[at, 0:half2] = blocks[:, 0:r2].reshape(some * r2, half2).astype(BF)
        v2f[at, half2:] = blocks[:, r2:].reshape(some * r2, half2).astype(BF)
        return 0

    lax.fori_loop(0, 2 * nx, turn_step, 0)

    came(11, ex5.at[pl.ds(0, nby - 1)])
    z2b = jnp.concatenate([ex5[j] for j in range(nby)], axis=1)

    y2 = nt(z2b, v2f[...]).astype(BF)
    s2 = nn(y2, v2f[...])
    s2o[...] = s2
    s2b = s2.astype(BF)
    back1 = s1y - nt(s2b, f)
    s1 = nn(back1.astype(BF), v1)
    s1o[...] = s1
    s1b = s1.astype(BF)
    for cols in tiles:
        ly[:, cols] = ly[:, cols] - nn(s1b, ct[:, cols]) - nn(s2b, et[:, cols])
    rest = ly[...].astype(BF)
    for cols in tiles:
        filt[:, cols] = nn(rest, gt[:, cols])

    if nz > 1:
        for k, _, rest_of in stage_z:
            went(k, rest_of)
    went(3, v2x.at[core, outer, pl.ds(0, ny - 1)])
    went(4, v2x.at[core, pl.ds(0, nx - 1)])
    for k, buf in ((5, ff), (6, vv), (7, v2x)):
        went(k, buf.at[core])
    went(8, ex1.at[pl.ds(0, nby - 1)])
    went(9, ex3.at[pl.ds(0, nby - 1)])
    went(10, ex4.at[pl.ds(0, nbx - 1)])
    went(11, ex5.at[pl.ds(0, nby - 1)])
    for gi in range(nx):
        n = gs - 1 if gi == last else gs
        got = packed.at[gi, pl.ds(0, n)]
        pltpu.make_async_copy(got, got, send_v.at[gi]).wait()
        got = rcell.at[gi, pl.ds(0, n)]
        pltpu.make_async_copy(got, got, send_c.at[gi]).wait()


def store(filt, s1, s2, filt_h, s1_h, s2_h, sem):
    copies = [
        pltpu.make_async_copy(src, dst, sem.at[k])
        for k, (src, dst) in enumerate(((filt, filt_h), (s1, s1_h), (s2, s2_h)))
    ]
    for cp in copies:
        cp.start()
    for cp in copies:
        cp.wait()


def body(nbx, nby, sens, owner, cell, g, c, e, f, v1, v2, rhs1, rhs2):
    nx = 4 if nbx == 16 else 2
    ny, nz = nbx // nx, nby // 2
    nd = nbx * nby
    gs = nd // nx
    rr, held = sens.shape
    ni = g.shape[1]
    ns1 = c.shape[1]
    ns2 = e.shape[1]
    vmem = pl.BlockSpec(memory_space=pltpu.VMEM)
    hbm = pl.BlockSpec(memory_space=pltpu.HBM)
    rows = max(gs // 2 * rr, 256)
    rhs2 = rhs2.T
    scratch = [
        pltpu.VMEM((rr, held), F32),
        pltpu.VMEM((1, held), I32),
        pltpu.VMEM((1, held), I32),
        pltpu.VMEM((ni, ni), BF),
        pltpu.VMEM((ni, ns1), BF),
        pltpu.VMEM((ni, ns2), BF),
        pltpu.VMEM((2, nz) + f.shape, BF),
        pltpu.VMEM((2, nz) + v1.shape, BF),
        pltpu.VMEM(v2.shape, BF),
        pltpu.VMEM(rhs1.shape, F32),
        pltpu.VMEM(rhs2.shape, F32),
        pltpu.VMEM((256, 128), BF),
        pltpu.VMEM((CHUNK, 2 * SLOTS), BF),
        pltpu.VMEM((CHUNK, CHUNK + 128), BF),
        pltpu.VMEM((held, 2 * SLOTS), BF),
        pltpu.VMEM((16, held), BF),
        pltpu.VMEM((rr, held), BF),
        pltpu.VMEM((rows, WIDE), BF),
        pltpu.VMEM((LAND, 256), BF),
        pltpu.VMEM((rows, 256), F32),
        pltpu.VMEM((nd, 256), F32),
        pltpu.VMEM((nd, 128), F32),
        pltpu.VMEM((nx, gs, rr, SLOTS), BF),
        pltpu.VMEM((nd, 1, SLOTS), F32),
        pltpu.VMEM((nx, gs, rr, SLOTS), BF),
        pltpu.VMEM((nx, gs, 1, SLOTS), F32),
        pltpu.VMEM((ni, ni), BF),
        pltpu.VMEM((ns1, ni), BF),
        pltpu.VMEM((ns2, ni), BF),
        pltpu.VMEM((rr, ni), F32),
        pltpu.VMEM((2, nx, ny, nz, 2 * v2.shape[0], ns2 // 2), BF),
        pltpu.VMEM((ns2, ns2), BF),
        pltpu.VMEM((128, 128), F32),
        pltpu.VMEM((rr, ns1), F32),
        pltpu.VMEM((rr, ns2), F32),
        pltpu.VMEM((nby, rr, ns1), BF),
        pltpu.VMEM((nby, rr, 128), BF),
        pltpu.VMEM((nby, rr, 128), BF),
        pltpu.VMEM((nbx, rr, 128), BF),
        pltpu.VMEM((nby, rr, 128), BF),
        pltpu.SemaphoreType.DMA((11,)),
        pltpu.SemaphoreType.DMA((nx,)),
        pltpu.SemaphoreType.DMA((nx,)),
        pltpu.SemaphoreType.DMA((nx,)),
        pltpu.SemaphoreType.DMA((nx,)),
        pltpu.SemaphoreType.DMA((13,)),
        pltpu.SemaphoreType.DMA((13,)),
    ]
    shapes = (
        jax.ShapeDtypeStruct((rr, ni), F32),
        jax.ShapeDtypeStruct((rr, ns1), F32),
        jax.ShapeDtypeStruct((rr, ns2), F32),
    )
    outs = pl.pallas_call(
        functools.partial(kernel, nbx, nby),
        out_shape=shapes,
        in_specs=[hbm] * 11,
        out_specs=(vmem,) * 3,
        scratch_shapes=scratch,
        compiler_params=pltpu.CompilerParams(
            collective_id=0, has_side_effects=True, vmem_limit_bytes=51 << 20
        ),
    )(*[
        pltpu.with_memory_space_constraint(v, pltpu.HBM) for v in (
            sens, owner.reshape(1, held), cell.reshape(1, held), g.reshape(ni, ni),
            c, e, f, v1, v2, rhs1, rhs2,
        )
    ])
    return pl.pallas_call(
        store,
        out_shape=shapes,
        in_specs=[vmem] * 3,
        out_specs=(hbm,) * 3,
        scratch_shapes=[pltpu.SemaphoreType.DMA((3,))],
        compiler_params=pltpu.CompilerParams(vmem_limit_bytes=2 << 20),
    )(*outs)


def solution(mesh):
    nbx, nby = mesh.shape["bx"], mesh.shape["by"]
    both = ("bx", "by")
    in_specs = (
        P(None, both), P(both, None), P(both), P(both, None, None),
        P(both, None), P(both, None), P(both, None), P(both, None), P(both, None),
        P(None, both), P(None, both),
    )
    out_specs = (P(None, both), P(None, "bx"), P())
    return jax.shard_map(
        functools.partial(body, nbx, nby), mesh=mesh, in_specs=in_specs, out_specs=out_specs,
        check_vma=False,
    )
```
